512 devices in a mesh: seq: 128 (over z, y, core), tp: 4 (over x).
Axes of the slice: x: 4, y: 4, z: 16, core: 2. Of those that a mesh axis runs over, the one named last changes fastest.
Arguments:
- tokens: bfloat16 [16384, 1024], P('seq'), may hold values from -6 to 6
- norm_gain: float32 [1024], replicated, may hold values from 0.25 to 1.75
- w_qkv: bfloat16 [1024, 3, 1024], P(None, None, 'tp'), may hold values from -1 to 1
- w_out: bfloat16 [1024, 1024], P('tp'), may hold values from -0.1875 to 0.1875
- head_bias: float32 [2, 16], P(None, 'tp'), may hold values from -1.5 to 1.5
- kv_pool: bfloat16 [512, 128, 2, 1024], P('seq', None, None, 'tp'), may hold values from -6 to 6
- key_variate: int32 [512, 128], P('seq'), may hold values from 0 to 7
- page_table: int32 [128, 4], P('seq'), may hold values from 0 to 3, each once within a row
- node_len: int32 [128], P('seq'), may hold values from 1 to 512, 49152 in all
- path_nodes: int32 [16384, 3], P('seq'), may hold values from 0 to 127, all different within a row; in each aligned block of 128 rows (0 to 127, 128 to 255, ...) at most 8 rows name the same one
- query_variate: int32 [16384], P('seq'), may hold values from 0 to 7
Outputs:
- updated: bfloat16 [16384, 1024], P('seq')
The draws below stay inside these ranges and needn't reach their ends.
Inputs may be any that keep to these rules, and one draw needn't show every extreme that they name: `path_nodes`: each row names three different nodes; the rows of one device name one node at most 8 times, a bound that some block reaches. `page_table`: each row is a permutation. `node_len`: some node holds exactly 512 tokens.
All inputs are finite; a program needn't handle non-finite values. No bound on the sum of `node_len` on one device may be relied on, other than what follows from the above.
Results may differ from the reference program's by a relative error of at most 0.0033.
The reference program's roundings to bfloat16 on the way count: a program that leaves them out, or rounds other values in their place, can miss the bound.
Values may be sent and summed in bfloat16 or wider, within the bound.
A program may use at most 64 MiB of HBM per device.

```python
import math
import jax
import jax.numpy as jnp
import numpy as np
from jax import lax

D = 1024
H = 16
HD = 64
TOK_DEV = 128
PAGE = 128
PAGES_NODE = 4
VARIATES = 8
NODE_LEN = 512
CAP = 8
TOKENS = 16384
N_SEQ = 128


def draw_w_qkv(key, part):
    first = jax.random.fold_in(key, 11)
    base = jnp.clip(jax.random.normal(first, (D, 3, H * HD), jnp.float32), -4.0, 4.0) * D ** (-0.5)
    return base.astype(jnp.bfloat16)


def draw_kv_pool(key, part):
    rows = N_SEQ * PAGES_NODE
    first = jax.random.fold_in(key, 21)
    third = jax.random.fold_in(key, 23)
    values = jnp.clip(jax.random.normal(third, (rows, PAGE, H * HD), jnp.float32), -6.0, 6.0)
    keys = jnp.clip(jax.random.normal(first, (rows, PAGE, H * HD), jnp.float32), -6.0, 6.0)
    return jnp.stack([keys, values], axis=2).astype(jnp.bfloat16)


def place_ends(result, stream_key, low, high):
    dims = result.shape
    index_at = [jax.random.randint(jax.random.fold_in(stream_key, axis), (), 0, dims[axis]) for axis in range(len(dims))]
    result = result.at[tuple(index_at)].set(low)
    longest = dims.index(max(dims))
    index_at[longest] = (index_at[longest] + 1) % dims[longest]
    return result.at[tuple(index_at)].set(high)


def level_of(stream_key, shape, pieces, least, high):
    level, own = 1.0, jax.random.fold_in(stream_key, 6)
    for position, blocks in pieces:
        steps = jnp.exp(jax.random.uniform(jax.random.fold_in(own, position), (blocks,), jnp.float32, least / len(pieces), high / len(pieces)))
        level = level * jnp.repeat(steps, shape[position] // blocks).reshape([-1 if axis == position else 1 for axis in range(len(shape))])
    return level


def length_profile(count, total, most, skew):
    loads = [(1 << 20) // math.isqrt(grade ** skew) + 1 for grade in range(2, count + 1)]
    rest, given = total - most - (count - 1), [1] * (count - 1)
    while rest > 0:
        candidates = [i for i in range(count - 1) if given[i] < most]
        whole, left = sum([loads[i] for i in candidates]), rest
        for i in candidates:
            addition = min(most - given[i], max(1, left * loads[i] // whole), rest)
            given[i] = given[i] + addition
            rest = rest - addition
    return np.array([most] + given)


def uneven(rng, number_of, total, bound, skew):
    if number_of == 2:
        one = jax.random.randint(rng, (), max(1, total - bound), min(bound, total - 1) + 1)
        return jnp.stack([one, total - one])
    lengths = jnp.asarray(length_profile(number_of, total, bound, skew), jnp.int32)
    twos = (number_of - 1) // 2
    donor, sink = lengths[1:1 + 2 * twos:2], lengths[2:2 + 2 * twos:2]
    room = jnp.minimum(donor - 1, bound - sink)
    shifted = jax.random.randint(jax.random.fold_in(rng, 1), (twos,), 0, 1 << 20) % (room + 1)
    lengths = lengths.at[1:1 + 2 * twos:2].set(donor - shifted).at[2:2 + 2 * twos:2].set(sink + shifted)
    return lengths[jax.random.permutation(jax.random.fold_in(rng, 2), number_of)]


def assign_block(own_key, own, number, rows, number_of, top, bound, slope):
    sequence = jax.random.permutation(own_key, number_of)
    heavy_load, usual = load_shares(number_of, rows * top, bound, slope, True), load_shares(number_of, rows * top, bound, slope, False)
    places = jnp.arange(number_of)

    def named(tallies, turn):
        used = int((tallies > 0).sum())
        fixed = max(1, used // 4)
        moved = fixed + (places - fixed + turn * (used - fixed)) % max(1, number_of - fixed)
        return jnp.zeros((number_of,), jnp.int32).at[sequence[jnp.where(places < fixed, places, moved)]].set(jnp.asarray(tallies, jnp.int32))

    tallies = jnp.where(number % 4 == 0, named(heavy_load, number // 4), named(usual, number - number // 4 - 1))
    mixed = jax.random.permutation(jax.random.fold_in(own, 3), number_of)
    donor, taker = mixed[0:number_of // 2 * 2:2], mixed[1:number_of // 2 * 2:2]
    slack = jnp.minimum(tallies[donor] - 1, bound - tallies[taker]) // 2
    slack = jnp.where((donor == sequence[0]) | (taker == sequence[0]) | (tallies[taker] == 0), 0, jnp.maximum(slack, 0))
    moved = jax.random.randint(jax.random.fold_in(own, 4), (number_of // 2,), 0, 1 << 20) % (slack + 1)
    tallies = tallies.at[donor].add(-moved).at[taker].add(moved)
    members = jnp.searchsorted(jnp.cumsum(tallies), jnp.arange(rows * top), side="right").astype(jnp.int32)
    grid = members.reshape(top, rows).T
    grid = grid[jax.random.permutation(jax.random.fold_in(own, 1), rows)]
    turn = jax.random.randint(jax.random.fold_in(own, 2), (rows, 1), 0, top)
    return jnp.take_along_axis(grid, (jnp.arange(top)[None, :] + turn) % top, axis=1)


def load_shares(amount, total, reach, slope, full):
    portions = [(1 << 20) // math.isqrt(grade ** slope) + 1 for grade in range(1, amount + 1)]
    largest = reach if full else min(reach, max(-(-total // amount), total * portions[0] // sum(portions)))
    least = 1 if total - largest >= amount - 1 else 0
    counts, surplus = [largest] + [least] * (amount - 1), total - largest - least * (amount - 1)
    while surplus > 0:
        free = [i for i in range(1, amount) if counts[i] < largest] or [i for i in range(1, amount) if counts[i] < reach]
        mass, budget = sum([portions[i] for i in free]), surplus
        for i in free:
            more = min(reach - counts[i], max(1, budget * portions[i] // mass), surplus)
            counts[i] = counts[i] + more
            surplus = surplus - more
    return np.array(counts)


def normal_values(key, shape, deviation, limit, split=(), held_as=jnp.bfloat16):
    loudness = level_of(key, shape, split, -0.22, 0.18) if split else 1.0
    result = jax.random.normal(key, shape, jnp.float32) * deviation * loudness
    return jnp.minimum(jnp.maximum(result, -limit), limit).astype(held_as)


def setup_inputs(seed: int = 0) -> dict:
    arg_keys = jax.random.split(jax.random.key(seed), 12)
    tokens = normal_values(arg_keys[0], (TOKENS, D), 1.0, 6.0, ((0, 128),))
    norm_gain = jnp.clip(1.0 + 0.15 * jax.random.normal(arg_keys[1], (D,), jnp.float32), 0.25, 1.75)
    w_qkv = draw_w_qkv(jax.random.fold_in(arg_keys[11], 71), 0)
    w_out = normal_values(arg_keys[3], (H * HD, D), (H * HD) ** -0.5, 0.1875, ((0, 4),))
    head_bias = jnp.clip(jax.random.uniform(arg_keys[4], (2, H), jnp.float32, -1.5, 1.5) * level_of(arg_keys[4], (2, H), ((1, 4),), -0.4, 0.0), -1.5, 1.5)
    kv_pool = draw_kv_pool(jax.random.fold_in(arg_keys[11], 71), 0)
    key_variate = place_ends(jax.random.randint(arg_keys[6], (N_SEQ * PAGES_NODE, PAGE), 0, VARIATES), jax.random.fold_in(arg_keys[6], 1), 0, VARIATES - 1).astype(jnp.int32)
    page_table = jax.vmap(lambda own: jax.random.permutation(own, PAGES_NODE))(jax.random.split(arg_keys[7], N_SEQ)).reshape((N_SEQ, PAGES_NODE)).astype(jnp.int32)
    node_len = uneven(arg_keys[8], N_SEQ, N_SEQ * NODE_LEN * 3 // 4, NODE_LEN, 2).astype(jnp.int32)
    path_nodes_keys = jax.random.split(jax.random.fold_in(arg_keys[9], 1), TOKENS // TOK_DEV)
    path_nodes_turns = jax.random.permutation(jax.random.fold_in(arg_keys[9], 3), TOKENS // TOK_DEV)
    path_nodes = jax.vmap(lambda own, number: assign_block(jax.random.fold_in(arg_keys[9], 2), own, number, TOK_DEV, N_SEQ, 3, CAP, 2))(path_nodes_keys, path_nodes_turns).reshape((TOKENS, 3))
    query_variate = place_ends(jax.random.randint(arg_keys[10], (TOKENS,), 0, VARIATES), jax.random.fold_in(arg_keys[10], 1), 0, VARIATES - 1).astype(jnp.int32)
    return {"tokens": tokens, "norm_gain": norm_gain, "w_qkv": w_qkv, "w_out": w_out, "head_bias": head_bias, "kv_pool": kv_pool, "key_variate": key_variate, "page_table": page_table, "node_len": node_len, "path_nodes": path_nodes, "query_variate": query_variate}


def head_attend(qh, kh, vh, same, bias_same, bias_diff, valid):
    scores = jnp.dot(qh, kh.T, preferred_element_type=jnp.float32) * HD ** (-0.5)
    scores = scores + jnp.where(same, bias_same, bias_diff)
    scores = jnp.where(valid[None, :], scores, -1e+30)
    peak = lax.optimization_barrier(jnp.max(scores, axis=1))
    weights = jnp.exp(scores - peak[:, None])
    total = lax.optimization_barrier(jnp.sum(weights, axis=1))
    mixed = jnp.dot(weights.astype(jnp.bfloat16), vh, preferred_element_type=jnp.float32) / total[:, None]
    mixed = lax.optimization_barrier(mixed.astype(jnp.bfloat16))
    return (mixed, peak, total)

def reference(tokens, norm_gain, w_qkv, w_out, head_bias, kv_pool, key_variate, page_table, node_len, path_nodes, query_variate):
    xf = tokens.astype(jnp.float32)
    normed = (xf * lax.rsqrt(lax.optimization_barrier(jnp.mean(xf * xf, axis=1, keepdims=True)) + 1e-05) * norm_gain).astype(jnp.bfloat16)
    qkv = jnp.dot(normed, w_qkv.reshape(D, 3 * H * HD), preferred_element_type=jnp.float32).astype(jnp.bfloat16)
    qkv = qkv.reshape(TOKENS, 3, H, HD)
    query, key, value = (qkv[:, 0], qkv[:, 1], qkv[:, 2])
    pool = kv_pool.reshape(N_SEQ, PAGES_NODE, PAGE, 2, H, HD)
    pool_var = key_variate.reshape(N_SEQ, PAGES_NODE, PAGE)
    flat = path_nodes.reshape(-1)
    items = 3 * TOKENS
    recv = N_SEQ * CAP
    heads_q = jnp.moveaxis(query, 1, 0)

    def one_node(n, carry):
        outs, peaks, totals = carry
        order = lax.dynamic_index_in_dim(page_table, n, 0, keepdims=False)
        pages = lax.dynamic_index_in_dim(pool, n, 0, keepdims=False)[order].reshape(NODE_LEN, 2, H, HD)
        kvar = lax.dynamic_index_in_dim(pool_var, n, 0, keepdims=False)[order].reshape(NODE_LEN)
        length = lax.dynamic_index_in_dim(node_len, n, 0, keepdims=False)
        valid = jnp.arange(NODE_LEN, dtype=jnp.int32) < length
        hits = flat == n
        count = jnp.sum(hits.astype(jnp.int32))
        where_at = jnp.nonzero(hits, size=recv, fill_value=0)[0].astype(jnp.int32)
        rows = where_at // 3
        qvar = query_variate[rows]
        same = qvar[:, None] == kvar[None, :]
        qn = heads_q[:, rows]
        kn = jnp.moveaxis(pages[:, 0], 1, 0)
        vn = jnp.moveaxis(pages[:, 1], 1, 0)

        def per_head(xs):
            return head_attend(xs[0], xs[1], xs[2], same, xs[3], xs[4], valid)
        mixed, peak, total = lax.map(per_head, (qn, kn, vn, head_bias[1], head_bias[0]))
        ok = jnp.arange(recv, dtype=jnp.int32) < count
        target = jnp.where(ok, where_at, items).astype(jnp.int32)
        outs = outs.at[target].set(jnp.moveaxis(mixed, 0, 1).astype(jnp.float32), mode='drop')
        peaks = peaks.at[target].set(peak.T, mode='drop')
        totals = totals.at[target].set(total.T, mode='drop')
        return (outs, peaks, totals)
    start = (jnp.zeros((items, H, HD), jnp.float32), jnp.zeros((items, H), jnp.float32), jnp.ones((items, H), jnp.float32))
    outs, peaks, totals = lax.fori_loop(0, N_SEQ, one_node, start)
    own_peak = lax.optimization_barrier(jnp.sum(query.astype(jnp.float32) * key.astype(jnp.float32), axis=2)) * HD ** (-0.5) + head_bias[1][None, :]
    all_o = jnp.concatenate([value.astype(jnp.float32)[:, None], outs.reshape(TOKENS, 3, H, HD)], axis=1)
    all_m = jnp.concatenate([own_peak[:, None], peaks.reshape(TOKENS, 3, H)], axis=1)
    all_l = jnp.concatenate([jnp.ones((TOKENS, 1, H), jnp.float32), totals.reshape(TOKENS, 3, H)], axis=1)
    top = lax.optimization_barrier(jnp.max(all_m, axis=1, keepdims=True))
    scale = all_l * jnp.exp(all_m - top)
    attn = (lax.optimization_barrier(jnp.sum(scale[..., None] * all_o, axis=1)) / lax.optimization_barrier(jnp.sum(scale, axis=1))[..., None]).astype(jnp.bfloat16)
    projected = jnp.dot(attn.reshape(TOKENS, H * HD), w_out, preferred_element_type=jnp.float32)
    return (xf + projected).astype(jnp.bfloat16)
```

```python
import functools

import jax
import jax.numpy as jnp
from jax import lax
from jax.experimental import pallas as pl
from jax.experimental.pallas import tpu as pltpu
from jax.sharding import PartitionSpec as P

HD = 64
CAP = 8
MESH = pl.DeviceIdType.MESH
NT = (((1,), (1,)), ((), ()))
F32, BF16, I32 = jnp.float32, jnp.bfloat16, jnp.int32


def iota(shape, axis):
    return lax.broadcasted_iota(I32, shape, axis)


def kernel(
    dims,
    qkv_ref, x_ref, w_ref, bias_ref, k_ref, v_ref, kvar_ref, pt_ref, len_ref, path_ref, qvar_ref,
    out_ref,
    qall, meta, psend, prec, rsend, rrec, ssend, srec, zsend, zrec, zsrec,
    kext, vt, wall, attn, fb, acc_o, acc_s, own_m,
    ring_s, ring_r, meta_s, meta_r, p_s, p_r, r_s, r_r, st_s, st_r, z_s, z_r, zs_s, zs_r,
    w_s, w_r, a_s, a_r, local_s,
):
    NZ, NP, TP = dims
    NS = NZ // 2
    T = x_ref.shape[0]
    cols = k_ref.shape[1]
    heads = cols // HD
    keys = k_ref.shape[0]
    pages, page = kvar_ref.shape
    nodes = NZ * NP
    R = NP * 2 * CAP
    half = NP * CAP

    s = lax.axis_index("seq")
    t = lax.axis_index("tp")
    z = s // NP
    p = s % NP

    def zdev(d):
        return (((z + d) % NZ) * NP + p, t)

    def pdev(d):
        return (z * NP + (p + d) % NP, t)

    def tdev(d):
        return (s, (t + d) % TP)

    barrier = pltpu.get_barrier_semaphore()
    for d in range(1, NZ):
        pl.semaphore_signal(barrier, inc=1, device_id=zdev(d), device_id_type=MESH)
    for d in range(1, NP):
        pl.semaphore_signal(barrier, inc=1, device_id=pdev(d), device_id_type=MESH)
    for d in range(1, TP):
        pl.semaphore_signal(barrier, inc=1, device_id=tdev(d), device_id_type=MESH)

    def rdma(src, dst, ss, rs, dev):
        return pltpu.make_async_remote_copy(
            src_ref=src, dst_ref=dst, send_sem=ss, recv_sem=rs, device_id=dev, device_id_type=MESH
        )

    path = path_ref[...]
    lane_n = iota((T, nodes), 1)
    hit = [path[:, j : j + 1] == lane_n for j in range(3)]
    hits = sum(h.astype(F32) for h in hit).astype(BF16)
    before = (iota((T, T), 0) > iota((T, T), 1)).astype(F32).astype(BF16)
    count = jnp.dot(before, hits, preferred_element_type=F32)
    packed = jnp.zeros((T, 128), F32)
    lane = iota((T, 128), 1)
    for j in range(3):
        slot = jnp.sum(jnp.where(hit[j], count, 0.0), axis=1, keepdims=True)
        flat = path[:, j : j + 1].astype(F32) * CAP + slot
        packed = jnp.where(lane == j, flat, packed)
        fb[j * T : (j + 1) * T, :] = jnp.broadcast_to(flat, (T, 2 * half)).astype(I32)
    rows = packed.T.astype(I32)
    qall[NS - 1, 0] = qkv_ref[:, 0:cols]
    meta[NS - 1, 0] = jnp.concatenate([rows[0:3], qvar_ref[...]], axis=0)

    pl.semaphore_wait(barrier, NZ + NP + TP - 3)

    def ring(k):
        copies = []
        for way in range(2):
            dev = zdev(1 - 2 * way)
            src = (NS - 1, 0) if k == 1 else (k - 2, way)
            if k < NS:
                copies.append(rdma(qall.at[src], qall.at[k - 1, way], ring_s.at[way, k - 1], ring_r.at[way, k - 1], dev))
                copies.append(rdma(meta.at[src], meta.at[k - 1, way], meta_s.at[way, k - 1], meta_r.at[way, k - 1], dev))
            else:
                part = pl.ds(way * (T // 2), T // 2)
                copies.append(
                    rdma(qall.at[src + (part,)], qall.at[NS - 1, 1, part], ring_s.at[way, k - 1], ring_r.at[way, k - 1], dev)
                )
                if way == 0:
                    copies.append(rdma(meta.at[src], meta.at[NS - 1, 1], meta_s.at[0, k - 1], meta_r.at[0, k - 1], dev))
        return copies

    started = []

    def start(copies):
        for c in copies:
            c.start()
        started.extend(copies)
        return copies

    ring_now = start(ring(1))
    w_copies = start([rdma(w_ref, wall.at[t], w_s.at[d - 1], w_r.at[d - 1], tdev(d)) for d in range(1, TP)])
    w_local = pltpu.make_async_copy(w_ref, wall.at[t], local_s)
    w_local.start()

    length = len_ref[0]
    lane_p = iota((1, page), 1)
    var = kvar_ref[...]
    kk = k_ref[...].astype(F32) * HD ** (-0.5)
    head_of_lane = iota((keys, cols), 1) // HD
    sub = iota((128, page), 0)
    for h in range(heads):
        kext[h, :, 0:cols] = jnp.where(head_of_lane == h, kk, 0.0).astype(BF16)
        other, same = bias_ref[0, h], bias_ref[1, h]
        for g in range(pages):
            place = sum(jnp.where(pt_ref[0, i] == g, i, 0) for i in range(pages))
            valid = place * page + lane_p < length
            b = jnp.where(var[g : g + 1] == sub % 8, same, other)
            hi = b.astype(BF16).astype(F32)
            mid = (b - hi).astype(BF16).astype(F32)
            low = b - hi - mid
            piece = jnp.where(sub < 8, jnp.where(valid, hi, -1e30), jnp.where(valid, jnp.where(sub < 16, mid, low), 0.0))
            piece = jnp.where(sub < 24, piece, 0.0)
            kext[h, g * page : (g + 1) * page, cols : cols + 128] = piece.T.astype(BF16)
    vt[...] = v_ref[...].astype(F32).T.astype(BF16)

    prod = qkv_ref[:, 0:cols].astype(F32) * qkv_ref[:, cols : 2 * cols].astype(F32)
    own_m[...] = jnp.concatenate(
        [jnp.sum(prod[:, h * HD : (h + 1) * HD], axis=1, keepdims=True) * HD ** (-0.5) + bias_ref[1, h] for h in range(heads)],
        axis=1,
    )
    acc_o[...] = jnp.zeros_like(acc_o)
    acc_s[...] = jnp.zeros_like(acc_s)

    row = iota((R, 1), 0)
    target = (z * NP + row // (2 * CAP)) * CAP + row % CAP
    which = (row // CAP) % 2
    sub_t = iota((128, T), 0)

    def select(i):
        sel, one = [], []
        for b in range(2):
            m = meta[i, b]
            want = jnp.where(which == b, target, -1)
            got = (m[0:1] == want) | (m[1:2] == want) | (m[2:3] == want)
            sel.append(got.astype(F32).astype(BF16))
            one.append(((m[3:4] == sub_t % 8) & (sub_t < 24)).astype(F32).astype(BF16))
        sel = jnp.concatenate(sel, axis=1)
        one = jnp.concatenate(one, axis=1)
        q = jnp.concatenate([qall[i, 0], qall[i, 1]], axis=0)
        qs = jnp.dot(sel, q, preferred_element_type=F32)
        os = lax.dot_general(sel, one, NT, preferred_element_type=F32)
        psend[i, :, :, :, 0:cols] = qs.reshape(NP, 2, CAP, cols).astype(BF16)
        psend[i, :, :, :, cols : cols + 128] = os.reshape(NP, 2, CAP, 128).astype(BF16)
        prec[i, p] = psend[i, p]
        return start(
            [
                rdma(psend.at[i, (p + d) % NP], prec.at[i, p], p_s.at[i, d - 1], p_r.at[i, d - 1], pdev(d))
                for d in range(1, NP)
            ]
        )

    def attend(i, copies):
        for c in copies:
            c.wait_recv()
        rows_q = prec[i].astype(F32).reshape(R, cols + 128).astype(BF16)
        outs, peaks, totals = [], [], []
        for h in range(heads):
            score = lax.dot_general(kext[h], rows_q, NT, preferred_element_type=F32)
            peak = jnp.max(score, axis=0, keepdims=True)
            weight = jnp.exp(score - peak)
            peaks.append(peak)
            totals.append(jnp.sum(weight, axis=0, keepdims=True))
            outs.append(
                jnp.dot(vt[h * HD : (h + 1) * HD, :], weight.astype(BF16), preferred_element_type=F32)
            )
        out = jnp.concatenate(outs, axis=0).T
        rsend[i] = out.reshape(NP, 2, CAP, cols).astype(BF16)
        ssend[i] = jnp.concatenate(peaks + totals, axis=0)
        rrec[i, p] = rsend[i, p]
        srec[i, p] = ssend[i]
        back = []
        for d in range(1, NP):
            back.append(rdma(rsend.at[i, (p + d) % NP], rrec.at[i, p], r_s.at[i, d - 1], r_r.at[i, d - 1], pdev(d)))
            back.append(rdma(ssend.at[i], srec.at[i, p], st_s.at[i, d - 1], st_r.at[i, d - 1], pdev(d)))
        return start(back)

    lane_r = iota((8, R), 1)

    def give_back(i, copies):
        for c in copies:
            c.wait_recv()
        home = []
        for b in range(2):
            acc = jnp.zeros((8, R), F32)
            for o in range(NP):
                tile = srec[i, o]
                shift = (o * CAP + R - p * 2 * CAP - b * CAP + R) % R
                acc = jnp.where(lane_r // CAP == o, pltpu.roll(tile, shift, 1), acc)
            moved = pltpu.roll(acc, half, 1)
            both = jnp.where(lane_r[0:heads] < half, acc[0:heads], moved[heads : 2 * heads])
            if i == NS - 1 and b == 0:
                zrec[i, 0] = rrec[i, :, 0]
                zsrec[i, 0] = both
                continue
            zsend[i, b] = both
            dev = zdev(NS) if i == NS - 1 else zdev((2 * b - 1) * (i + 1))
            home.append(rdma(rrec.at[i, :, b], zrec.at[i, b], z_s.at[i, b], z_r.at[i, b], dev))
            home.append(rdma(zsend.at[i, b], zsrec.at[i, b], zs_s.at[i, b], zs_r.at[i, b], dev))
        return start(home)

    lane_g = iota((3 * T, 2 * half), 1)
    lane_h = iota((heads, 2 * half), 1)

    def collect(i, copies):
        for c in copies:
            c.wait_recv()
        if i == NS - 1:
            first, second = z, (z + NS) % NZ
        else:
            first, second = (z + i + 1) % NZ, (z + NZ - i - 1) % NZ
        want = jnp.where(lane_g < half, first * half + lane_g, second * half + lane_g - half)
        pick = (fb[...] == want).astype(F32)
        both = zrec[i].astype(F32).reshape(2 * half, cols).astype(BF16)
        acc_o[...] += jnp.dot(pick.astype(BF16), both, preferred_element_type=F32)
        s0, s1 = zsrec[i, 0], zsrec[i, 1]
        m = jnp.where(lane_h < half, s0, pltpu.roll(s1, half, 1))
        l = jnp.where(lane_h < half, pltpu.roll(s0, half, 1), s1)
        stats = jnp.concatenate([m, l], axis=0)
        acc_s[...] += lax.dot_general(
            pick, stats, NT, precision=lax.Precision.HIGHEST, preferred_element_type=F32
        )

    sent, back, home = {}, {}, {}
    for k in range(1, NS + 3):
        if k <= NS:
            for c in ring_now:
                c.wait_recv()
            if k < NS:
                ring_now = start(ring(k + 1))
            sent[k - 1] = select(k - 1)
        if 0 <= k - 2 < NS:
            back[k - 2] = attend(k - 2, sent[k - 2])
        if 0 <= k - 3 < NS:
            home[k - 3] = give_back(k - 3, back[k - 3])
    for i in range(NS):
        collect(i, home[i])

    m0 = own_m[...]
    ms = [acc_s[j * T : (j + 1) * T, 0:heads] for j in range(3)]
    ls = [acc_s[j * T : (j + 1) * T, heads : 2 * heads] for j in range(3)]
    top = jnp.maximum(jnp.maximum(m0, ms[0]), jnp.maximum(ms[1], ms[2]))
    w0 = jnp.exp(m0 - top)
    ws = [jnp.exp(m - top) for m in ms]
    den = w0 + ws[0] * ls[0] + ws[1] * ls[1] + ws[2] * ls[2]

    def wide(c):
        return jnp.concatenate([jnp.broadcast_to(c[:, h : h + 1], (T, HD)) for h in range(heads)], axis=1)

    mixed = wide(w0) * qkv_ref[:, 2 * cols : 3 * cols].astype(F32)
    for j in range(3):
        mixed = mixed + wide(ws[j]) * acc_o[j * T : (j + 1) * T, :]
    mixed = mixed / wide(den)
    attn[t] = mixed.astype(BF16)
    a_copies = start(
        [rdma(attn.at[t], attn.at[t], a_s.at[d - 1], a_r.at[d - 1], tdev(d)) for d in range(1, TP)]
    )
    w_local.wait()
    for c in w_copies:
        c.wait_recv()
    for c in a_copies:
        c.wait_recv()
    total = jnp.zeros(out_ref.shape, F32)
    for j in range(TP):
        total = total + jnp.dot(attn[j], wall[j], preferred_element_type=F32)
    out_ref[...] = (x_ref[...].astype(F32) + total).astype(BF16)
    for c in started:
        c.wait_send()


def body(
    dims,
    tokens,
    norm_gain,
    w_qkv,
    w_out,
    head_bias,
    kv_pool,
    key_variate,
    page_table,
    node_len,
    path_nodes,
    query_variate,
):
    NZ, NP, TP = dims
    NS = NZ // 2
    T, width = tokens.shape
    cols = w_qkv.shape[2]
    heads = cols // HD
    pages, page = key_variate.shape
    keys = pages * page
    R = NP * 2 * CAP
    half = NP * CAP
    xf = tokens.astype(F32)
    normed = (xf * lax.rsqrt(jnp.mean(xf * xf, axis=1, keepdims=True) + 1e-05) * norm_gain).astype(BF16)
    qkv = jnp.dot(normed, w_qkv.reshape(width, 3 * cols), preferred_element_type=F32).astype(BF16)
    k = kv_pool[:, :, 0].reshape(keys, cols)
    v = kv_pool[:, :, 1].reshape(keys, cols)
    vmem = pl.BlockSpec(memory_space=pltpu.VMEM)
    smem = pl.BlockSpec(memory_space=pltpu.SMEM)
    dma = pltpu.SemaphoreType.DMA
    scratch = [
        pltpu.VMEM((NS, 2, T, cols), BF16),
        pltpu.VMEM((NS, 2, 4, T), I32),
        pltpu.VMEM((NS, NP, 2, CAP, cols + 128), BF16),
        pltpu.VMEM((NS, NP, 2, CAP, cols + 128), BF16),
        pltpu.VMEM((NS, NP, 2, CAP, cols), BF16),
        pltpu.VMEM((NS, NP, 2, CAP, cols), BF16),
        pltpu.VMEM((NS, 8, R), F32),
        pltpu.VMEM((NS, NP, 8, R), F32),
        pltpu.VMEM((NS, 2, heads, R), F32),
        pltpu.VMEM((NS, 2, NP, CAP, cols), BF16),
        pltpu.VMEM((NS, 2, heads, R), F32),
        pltpu.VMEM((heads, keys, cols + 128), BF16),
        pltpu.VMEM((cols, keys), BF16),
        pltpu.VMEM((TP,) + w_out.shape, BF16),
        pltpu.VMEM((TP, T, cols), BF16),
        pltpu.VMEM((3 * T, 2 * half), I32),
        pltpu.VMEM((3 * T, cols), F32),
        pltpu.VMEM((3 * T, 2 * heads), F32),
        pltpu.VMEM((T, heads), F32),
    ]
    sems = (
        [dma((2, NS))] * 4 + [dma((NS, NP - 1))] * 6 + [dma((NS, 2))] * 4 + [dma((TP - 1,))] * 4 + [dma(())]
    )
    return pl.pallas_call(
        functools.partial(kernel, dims),
        out_shape=jax.ShapeDtypeStruct((T, width), BF16),
        in_specs=[vmem, vmem, vmem, smem, vmem, vmem, vmem, smem, smem, vmem, vmem],
        out_specs=vmem,
        scratch_shapes=scratch + sems,
        compiler_params=pltpu.CompilerParams(
            collective_id=0, has_side_effects=True, vmem_limit_bytes=56 * 1024 * 1024
        ),
    )(
        qkv, tokens, w_out, head_bias, k, v, key_variate, page_table, node_len, path_nodes,
        query_variate.reshape(1, T),
    )


def build(mesh, plane):
    dims = (mesh.shape["seq"] // plane, plane, mesh.shape["tp"])
    in_specs = (
        P("seq", None),
        P(),
        P(None, None, "tp"),
        P("tp", None),
        P(None, "tp"),
        P("seq", None, None, "tp"),
        P("seq", None),
        P("seq", None),
        P("seq"),
        P("seq", None),
        P("seq"),
    )
    return jax.shard_map(
        functools.partial(body, dims), mesh=mesh, in_specs=in_specs, out_specs=P("seq", None), check_vma=False
    )


def solution(mesh):
    return build(mesh, 8)
```

```python
import functools

import jax
import jax.numpy as jnp
from jax import lax
from jax.experimental import pallas as pl
from jax.experimental.pallas import tpu as pltpu
from jax.sharding import PartitionSpec as P

HD = 64
CAP = 8
MESH = pl.DeviceIdType.MESH
NT = (((1,), (1,)), ((), ()))
F32, BF16, I32 = jnp.float32, jnp.bfloat16, jnp.int32


def iota(shape, axis):
    return lax.broadcasted_iota(I32, shape, axis)


def kernel(
    dims,
    x_hbm, gain_hbm, wqkv_hbm, w_hbm, bias_hbm, kv_hbm, kvar_hbm, pt_hbm, len_ref, path_hbm, qvar_hbm,
    out_ref,
    x_ref, gain_ref, wqkv_ref, bias_ref, kv_ref, kvar_ref, pt_ref, path_ref, qvar_ref, qkv,
    qall, meta, psend, prec, rsend, rrec, ssend, srec, zsend, zrec, zsrec,
    kext, vt, wall, attn, fb, acc_o, acc_s, own_m,
    ring_s, ring_r, meta_s, meta_r, p_s, p_r, r_s, r_r, st_s, st_r, z_s, z_r, zs_s, zs_r,
    w_s, w_r, a_s, a_r, local_s, in_s,
):
    NZ, NP, TP = dims
    NS = NZ // 2
    T = x_ref.shape[0]
    cols = wqkv_ref.shape[2]
    heads = cols // HD
    pages, page = kvar_ref.shape
    nodes = NZ * NP
    R = NP * 2 * CAP
    half = NP * CAP

    s = lax.axis_index("seq")
    t = lax.axis_index("tp")
    z = s // NP
    p = s % NP

    def zdev(d):
        return (((z + d) % NZ) * NP + p, t)

    def pdev(d):
        return (z * NP + (p + d) % NP, t)

    def tdev(d):
        return (s, (t + d) % TP)

    barrier = pltpu.get_barrier_semaphore()
    friends = [zdev(1), zdev(-1)] + [pdev(d) for d in range(1, NP)] + [tdev(d) for d in range(1, TP)]
    for dev in friends:
        pl.semaphore_signal(barrier, inc=1, device_id=dev, device_id_type=MESH)

    loads = {}
    pairs = dict(
        path=(path_hbm, path_ref), qvar=(qvar_hbm, qvar_ref), x=(x_hbm, x_ref), gain=(gain_hbm, gain_ref),
        w0=(wqkv_hbm.at[0], wqkv_ref.at[0]), w1=(wqkv_hbm.at[1], wqkv_ref.at[1]), w2=(wqkv_hbm.at[2], wqkv_ref.at[2]),
        kv=(kv_hbm, kv_ref), kvar=(kvar_hbm, kvar_ref), bias=(bias_hbm, bias_ref), pt=(pt_hbm, pt_ref),
        w=(w_hbm, wall.at[t]),
    )
    for j, (name, (src, dst)) in enumerate(pairs.items()):
        loads[name] = pltpu.make_async_copy(src, dst, in_s.at[j])
        loads[name].start()

    def rdma(src, dst, ss, rs, dev):
        return pltpu.make_async_remote_copy(
            src_ref=src, dst_ref=dst, send_sem=ss, recv_sem=rs, device_id=dev, device_id_type=MESH
        )

    loads["path"].wait()
    loads["qvar"].wait()
    path_rows = path_ref[...]
    path = jnp.concatenate([path_rows.astype(F32), jnp.zeros((5, T), F32)], axis=0).T.astype(I32)
    lane_n = iota((T, nodes), 1)
    hit = [path[:, j : j + 1] == lane_n for j in range(3)]
    hits = sum(h.astype(F32) for h in hit).astype(BF16)
    before = (iota((T, T), 0) > iota((T, T), 1)).astype(F32).astype(BF16)
    count = jnp.dot(before, hits, preferred_element_type=F32)
    packed = jnp.zeros((T, 128), F32)
    lane = iota((T, 128), 1)
    for j in range(3):
        slot = jnp.sum(jnp.where(hit[j], count, 0.0), axis=1, keepdims=True)
        flat = path[:, j : j + 1].astype(F32) * CAP + slot
        packed = jnp.where(lane == j, flat, packed)
        fb[j * T : (j + 1) * T, :] = jnp.broadcast_to(flat, (T, 2 * half)).astype(I32)
    rows = packed.T.astype(I32)
    meta[NS - 1, 0] = jnp.concatenate([rows[0:3], qvar_ref[...]], axis=0)
    loads["x"].wait()
    loads["gain"].wait()
    xf = x_ref[...].astype(F32)
    normed = (xf * lax.rsqrt(jnp.mean(xf * xf, axis=1, keepdims=True) + 1e-05) * gain_ref[...]).astype(BF16)
    loads["w0"].wait()
    qkv[0] = jnp.dot(normed, wqkv_ref[0], preferred_element_type=F32).astype(BF16)
    qall[NS - 1, 0] = qkv[0]

    pl.semaphore_wait(barrier, len(friends))

    def ring(k):
        copies = {}
        for way in range(2):
            dev = zdev(1 - 2 * way)
            src = (NS - 1, 0) if k == 1 else (k - 2, way)
            dst = (k - 1, way) if k < NS else (NS - 1, 1)
            if k < NS or way == 0:
                copies[way, "meta"] = rdma(meta.at[src], meta.at[dst], meta_s.at[way, k - 1], meta_r.at[way, k - 1], dev)
            for c in range(2):
                part = (pl.ds(c * (T // 2), T // 2),)
                if k < NS or way == c:
                    sems = (way, k - 1, c)
                    copies[way, c] = rdma(qall.at[src + part], qall.at[dst + part], ring_s.at[sems], ring_r.at[sems], dev)
        return copies

    started = []

    def start(copies):
        for c in copies:
            c.start()
        started.extend(copies)
        return copies

    ring_now = ring(1)
    start(list(ring_now.values()))
    w_copies = start([rdma(w_hbm, wall.at[t], w_s.at[d - 1], w_r.at[d - 1], tdev(d)) for d in range(1, TP)])
    for j in (1, 2):
        loads["w%d" % j].wait()
        qkv[j] = jnp.dot(normed, wqkv_ref[j], preferred_element_type=F32).astype(BF16)
    for name in ("kv", "kvar", "bias", "pt"):
        loads[name].wait()

    length = len_ref[0]
    lane_p = iota((1, page), 1)
    var = kvar_ref[...]
    sub = iota((128, page), 0)
    even = (iota((page, 2 * page), 1) == 2 * iota((page, 2 * page), 0)).astype(F32).astype(BF16)
    odd = (iota((page, 2 * page), 1) == 2 * iota((page, 2 * page), 0) + 1).astype(F32).astype(BF16)
    for g in range(pages):
        both = kv_ref[g].reshape(2 * page, cols)
        kk = jnp.dot(even, both, preferred_element_type=F32) * HD ** (-0.5)
        vt[:, g * page : (g + 1) * page] = jnp.dot(odd, both, preferred_element_type=F32).T.astype(BF16)
        place = sum(jnp.where(pt_ref[0, i] == g, i, 0) for i in range(pages))
        valid = place * page + lane_p < length
        for h in range(heads):
            other, same = bias_ref[0, h], bias_ref[1, h]
            b = jnp.where(var[g : g + 1] == sub % 8, same, other)
            hi = b.astype(BF16).astype(F32)
            mid = (b - hi).astype(BF16).astype(F32)
            low = b - hi - mid
            piece = jnp.where(sub < 72, jnp.where(valid, hi, -1e30), jnp.where(valid, jnp.where(sub < 80, mid, low), 0.0))
            piece = jnp.where((sub >= 64) & (sub < 88), piece, 0.0)
            kext[h, g * page : (g + 1) * page, :] = jnp.concatenate(
                [kk[:, h * HD : (h + 1) * HD], piece.T[:, HD:]], axis=1
            ).astype(BF16)

    prod = qkv[0].astype(F32) * qkv[1].astype(F32)
    own_m[...] = jnp.concatenate(
        [jnp.sum(prod[:, h * HD : (h + 1) * HD], axis=1, keepdims=True) * HD ** (-0.5) + bias_ref[1, h] for h in range(heads)],
        axis=1,
    )
    acc_o[...] = jnp.zeros_like(acc_o)
    acc_s[...] = jnp.zeros_like(acc_s)

    row = iota((R, 1), 0)
    target = (z * NP + row // (2 * CAP)) * CAP + row % CAP
    which = (row // CAP) % 2
    sub_t = iota((128, T), 0)

    def select(i):
        sel, one = [], []
        for b in range(2):
            m = meta[i, b]
            want = jnp.where(which == b, target, -1)
            got = (m[0:1] == want) | (m[1:2] == want) | (m[2:3] == want)
            sel.append(got.astype(F32).astype(BF16))
            one.append(((m[3:4] == sub_t % 8) & (sub_t >= 64) & (sub_t < 88)).astype(F32).astype(BF16))
        sel = jnp.concatenate(sel, axis=1)
        one = jnp.concatenate(one, axis=1)
        q = jnp.concatenate([qall[i, 0], qall[i, 1]], axis=0)
        qs = jnp.dot(sel, q, preferred_element_type=F32)
        os = lax.dot_general(sel, one, NT, preferred_element_type=F32)
        psend[i, :, :, :, 0:cols] = qs.reshape(NP, 2, CAP, cols).astype(BF16)
        psend[i, :, :, :, cols : cols + 128] = os.reshape(NP, 2, CAP, 128).astype(BF16)
        prec[i, p] = psend[i, p]
        return start(
            [
                rdma(psend.at[i, (p + d) % NP], prec.at[i, p], p_s.at[i, d - 1], p_r.at[i, d - 1], pdev(d))
                for d in range(1, NP)
            ]
        )

    lane_q = iota((R, 128), 1)

    def attend(i, copies):
        for c in copies:
            c.wait_recv()
        rows_q = prec[i].astype(F32).reshape(R, cols + 128)
        one = rows_q[:, cols : cols + 128]
        outs, peaks, totals = [], [], []
        for h in range(heads):
            pair = rows_q[:, h // 2 * 128 : h // 2 * 128 + 128]
            if h % 2:
                pair = pltpu.roll(pair, HD, 1)
            rows_h = jnp.where(lane_q < HD, pair, one).astype(BF16)
            score = lax.dot_general(kext[h], rows_h, NT, preferred_element_type=F32)
            peak = jnp.max(score, axis=0, keepdims=True)
            weight = jnp.exp(score - peak)
            peaks.append(peak)
            totals.append(jnp.sum(weight, axis=0, keepdims=True))
            outs.append(
                jnp.dot(vt[h * HD : (h + 1) * HD, :], weight.astype(BF16), preferred_element_type=F32)
            )
        out = jnp.concatenate(outs, axis=0).T
        rsend[i] = out.reshape(NP, 2, CAP, cols).astype(BF16)
        ssend[i] = jnp.concatenate(peaks + totals, axis=0)
        rrec[i, p] = rsend[i, p]
        srec[i, p] = ssend[i]
        back = []
        for d in range(1, NP):
            back.append(rdma(rsend.at[i, (p + d) % NP], rrec.at[i, p], r_s.at[i, d - 1], r_r.at[i, d - 1], pdev(d)))
            back.append(rdma(ssend.at[i], srec.at[i, p], st_s.at[i, d - 1], st_r.at[i, d - 1], pdev(d)))
        return start(back)

    lane_r = iota((8, R), 1)

    def give_back(i, copies):
        for c in copies:
            c.wait_recv()
        home = []
        for b in range(2):
            acc = jnp.zeros((8, R), F32)
            for o in range(NP):
                tile = srec[i, o]
                shift = (o * CAP + R - p * 2 * CAP - b * CAP + R) % R
                acc = jnp.where(lane_r // CAP == o, pltpu.roll(tile, shift, 1), acc)
            moved = pltpu.roll(acc, half, 1)
            both = jnp.where(lane_r[0:heads] < half, acc[0:heads], moved[heads : 2 * heads])
            if i == NS - 1 and b == 0:
                zrec[i, 0] = rrec[i, :, 0]
                zsrec[i, 0] = both
                continue
            zsend[i, b] = both
            dev = zdev(NS) if i == NS - 1 else zdev((2 * b - 1) * (i + 1))
            home.append(rdma(rrec.at[i, :, b], zrec.at[i, b], z_s.at[i, b], z_r.at[i, b], dev))
            home.append(rdma(zsend.at[i, b], zsrec.at[i, b], zs_s.at[i, b], zs_r.at[i, b], dev))
        return start(home)

    lane_g = iota((3 * T, 2 * half), 1)
    lane_h = iota((heads, 2 * half), 1)

    def collect(i, copies):
        for c in copies:
            c.wait_recv()
        if i == NS - 1:
            first, second = z, (z + NS) % NZ
        else:
            first, second = (z + i + 1) % NZ, (z + NZ - i - 1) % NZ
        want = jnp.where(lane_g < half, first * half + lane_g, second * half + lane_g - half)
        pick = (fb[...] == want).astype(F32)
        both = zrec[i].astype(F32).reshape(2 * half, cols).astype(BF16)
        acc_o[...] += jnp.dot(pick.astype(BF16), both, preferred_element_type=F32)
        s0, s1 = zsrec[i, 0], zsrec[i, 1]
        m = jnp.where(lane_h < half, s0, pltpu.roll(s1, half, 1))
        l = jnp.where(lane_h < half, pltpu.roll(s0, half, 1), s1)
        stats = jnp.concatenate([m, l], axis=0)
        acc_s[...] += lax.dot_general(
            pick, stats, NT, precision=lax.Precision.HIGHEST, preferred_element_type=F32
        )

    sent, back, home = {}, {}, {}
    for k in range(1, NS + 3):
        if k <= NS:
            ring_next = ring(k + 1) if k < NS else {}
            for what in ("meta", 0, 1):
                for way in range(2):
                    if (way, what) in ring_now:
                        ring_now[way, what].wait_recv()
                    if (way, what) in ring_next:
                        start([ring_next[way, what]])
            ring_now = ring_next
            sent[k - 1] = select(k - 1)
        if 0 <= k - 2 < NS:
            back[k - 2] = attend(k - 2, sent[k - 2])
        if 0 <= k - 3 < NS:
            home[k - 3] = give_back(k - 3, back[k - 3])
    for i in range(NS):
        collect(i, home[i])

    m0 = own_m[...]
    ms = [acc_s[j * T : (j + 1) * T, 0:heads] for j in range(3)]
    ls = [acc_s[j * T : (j + 1) * T, heads : 2 * heads] for j in range(3)]
    top = jnp.maximum(jnp.maximum(m0, ms[0]), jnp.maximum(ms[1], ms[2]))
    w0 = jnp.exp(m0 - top)
    ws = [jnp.exp(m - top) for m in ms]
    den = w0 + ws[0] * ls[0] + ws[1] * ls[1] + ws[2] * ls[2]

    def wide(c):
        return jnp.concatenate([jnp.broadcast_to(c[:, h : h + 1], (T, HD)) for h in range(heads)], axis=1)

    mixed = wide(w0) * qkv[2].astype(F32)
    for j in range(3):
        mixed = mixed + wide(ws[j]) * acc_o[j * T : (j + 1) * T, :]
    mixed = mixed / wide(den)
    attn[t] = mixed.astype(BF16)
    a_copies = start(
        [rdma(attn.at[t], attn.at[t], a_s.at[d - 1], a_r.at[d - 1], tdev(d)) for d in range(1, TP)]
    )
    loads["w"].wait()
    for c in w_copies:
        c.wait_recv()
    for c in a_copies:
        c.wait_recv()
    total = jnp.zeros(out_ref.shape, F32)
    for j in range(TP):
        total = total + jnp.dot(attn[j], wall[j], preferred_element_type=F32)
    out_ref[...] = (x_ref[...].astype(F32) + total).astype(BF16)
    for c in started:
        c.wait_send()


def body(
    dims,
    tokens,
    norm_gain,
    w_qkv,
    w_out,
    head_bias,
    kv_pool,
    key_variate,
    page_table,
    node_len,
    path_nodes,
    query_variate,
):
    NZ, NP, TP = dims
    NS = NZ // 2
    T, width = tokens.shape
    cols = w_qkv.shape[2]
    heads = cols // HD
    pages, page = key_variate.shape
    keys = pages * page
    R = NP * 2 * CAP
    half = NP * CAP
    vmem = pl.BlockSpec(memory_space=pltpu.VMEM)
    here = pl.BlockSpec(memory_space=pltpu.HBM)
    dma = pltpu.SemaphoreType.DMA
    scratch = [
        pltpu.VMEM((T, width), BF16),
        pltpu.VMEM((1, width), F32),
        pltpu.VMEM((3, width, cols), BF16),
        pltpu.SMEM(head_bias.shape, F32),
        pltpu.VMEM(kv_pool.shape, BF16),
        pltpu.VMEM((pages, page), I32),
        pltpu.SMEM(page_table.shape, I32),
        pltpu.VMEM((3, T), I32),
        pltpu.VMEM((1, T), I32),
        pltpu.VMEM((3, T, cols), BF16),
        pltpu.VMEM((NS, 2, T, cols), BF16),
        pltpu.VMEM((NS, 2, 4, T), I32),
        pltpu.VMEM((NS, NP, 2, CAP, cols + 128), BF16),
        pltpu.VMEM((NS, NP, 2, CAP, cols + 128), BF16),
        pltpu.VMEM((NS, NP, 2, CAP, cols), BF16),
        pltpu.VMEM((NS, NP, 2, CAP, cols), BF16),
        pltpu.VMEM((NS, 8, R), F32),
        pltpu.VMEM((NS, NP, 8, R), F32),
        pltpu.VMEM((NS, 2, heads, R), F32),
        pltpu.VMEM((NS, 2, NP, CAP, cols), BF16),
        pltpu.VMEM((NS, 2, heads, R), F32),
        pltpu.VMEM((heads, keys, 128), BF16),
        pltpu.VMEM((cols, keys), BF16),
        pltpu.VMEM((TP,) + w_out.shape, BF16),
        pltpu.VMEM((TP, T, cols), BF16),
        pltpu.VMEM((3 * T, 2 * half), I32),
        pltpu.VMEM((3 * T, cols), F32),
        pltpu.VMEM((3 * T, 2 * heads), F32),
        pltpu.VMEM((T, heads), F32),
    ]
    sems = (
        [dma((2, NS, 2))] * 2 + [dma((2, NS))] * 2 + [dma((NS, NP - 1))] * 6 + [dma((NS, 2))] * 4 + [dma((TP - 1,))] * 4 + [dma(()), dma((12,))]
    )
    call = pl.pallas_call(
        functools.partial(kernel, dims),
        out_shape=jax.ShapeDtypeStruct((T, width), BF16),
        in_specs=[here] * 8 + [pl.BlockSpec(memory_space=pltpu.SMEM)] + [here] * 2,
        out_specs=vmem,
        scratch_shapes=scratch + sems,
        compiler_params=pltpu.CompilerParams(
            collective_id=0, has_side_effects=True, vmem_limit_bytes=40 * 1024 * 1024
        ),
    )
    operands = (
        tokens, norm_gain.reshape(1, width), jnp.transpose(w_qkv, (1, 0, 2)), w_out, head_bias, kv_pool, key_variate,
        page_table, node_len, path_nodes.T, query_variate.reshape(1, T),
    )
    return call(*(a if a is node_len else pltpu.with_memory_space_constraint(a, pltpu.HBM) for a in operands))


def build(mesh, plane):
    dims = (mesh.shape["seq"] // plane, plane, mesh.shape["tp"])
    in_specs = (
        P("seq", None),
        P(),
        P(None, None, "tp"),
        P("tp", None),
        P(None, "tp"),
        P("seq", None, None, "tp"),
        P("seq", None),
        P("seq", None),
        P("seq"),
        P("seq", None),
        P("seq"),
    )
    return jax.shard_map(
        functools.partial(body, dims), mesh=mesh, in_specs=in_specs, out_specs=P("seq", None), check_vma=False
    )


def solution(mesh):
    return build(mesh, 8)
```
